32 devices in a mesh: mem: 8 (over z, x), grp: 4 (over y, core).
Axes of the slice: x: 2, y: 2, z: 4, core: 2. Of those that a mesh axis runs over, the one named last changes fastest.
Arguments:
- prior_members: bfloat16 [256, 32, 256], P('mem', 'grp'), may hold values from -6 to 6
- mapped_prior: bfloat16 [256, 32, 1024], P('mem', 'grp'), may hold values from -6 to 6
- departure: float32 [32, 1024], P(('grp', 'mem')), may hold values from -18 to 18
- precision_factor: float32 [32, 1024], P(('grp', 'mem')), may hold values from 0.02 to 0.5
- measured_lines: int32 [32], P(('grp', 'mem')), may hold values from 256 to 1024, as said below
Outputs:
- analysis: bfloat16 [256, 32, 256], P('mem', 'grp')
The draws below stay inside these ranges and needn't reach their ends.
Inputs may be any that keep to these rules, and one draw needn't show every extreme that they name: Only the first measured_lines rows of a patch's observation block are used; some patch has exactly 1024 rows and some exactly 256.
All inputs are finite; a program needn't handle non-finite values.
Results may differ from the reference program's by a relative error of at most 0.008.
Values may be sent and summed in bfloat16 or wider, within the bound.
No kernel may reach another device: no remote copies, remote signals or barrier semaphores. Data moves between devices by JAX's collectives and lax.ppermute only.
A program may use at most 64 MiB of HBM per device.

```python
import math
import jax
import jax.numpy as jnp
from jax import lax

MEMBER_NUMBER = 256
DOMAIN_UNKNOWNS = 256
OBS_MAX = 1024
ITERS = 5
DOMAIN_NUMBER = 32


def draw_measured_lines(key, part):
    lowest = OBS_MAX // 4
    spread = OBS_MAX - lowest
    key_rows = jax.random.fold_in(key, 11)
    key_high = jax.random.fold_in(key, 12)
    key_low = jax.random.fold_in(key, 13)
    draws = jax.random.randint(key_rows, (DOMAIN_NUMBER,), 0, spread + 1, dtype=jnp.int32)
    squared = draws * draws // spread
    counts = lowest + squared * draws // spread
    high_pos = jax.random.randint(key_high, (), 0, DOMAIN_NUMBER, dtype=jnp.int32)
    low_pos = (high_pos + 1 + jax.random.randint(key_low, (), 0, DOMAIN_NUMBER - 1, dtype=jnp.int32)) % DOMAIN_NUMBER
    positions = jnp.arange(DOMAIN_NUMBER, dtype=jnp.int32)
    counts = jnp.where(positions == high_pos, OBS_MAX, counts)
    counts = jnp.where(positions == low_pos, lowest, counts)
    return counts.astype(jnp.int32)


def block_scale(rng, extent, split, smallest, top_value):
    factor_of, own = 1.0, jax.random.fold_in(rng, 6)
    for dim, parts in split:
        steps = jnp.exp(jax.random.uniform(jax.random.fold_in(own, dim), (parts,), jnp.float32, smallest / len(split), top_value / len(split)))
        factor_of = factor_of * jnp.repeat(steps, extent[dim] // parts).reshape([-1 if axis == dim else 1 for axis in range(len(extent))])
    return factor_of


def normal_values(stream_key, dims, width, bound, shards=(), kind=jnp.bfloat16):
    drawn = jax.random.normal(stream_key, dims, jnp.float32) * width
    if len(shards) > 0:
        drawn = block_scale(stream_key, dims, shards, -0.22, 0.18) * drawn
    return jnp.clip(drawn, min=-bound, max=bound).astype(kind)


def setup_inputs(seed: int = 0) -> dict:
    seeds = jax.random.split(jax.random.key(seed), 6)
    prior_members = normal_values(seeds[0], (MEMBER_NUMBER, DOMAIN_NUMBER, DOMAIN_UNKNOWNS), 1.0, 6.0, ((0, 8), (1, 4)))
    mapped_prior = normal_values(seeds[1], (MEMBER_NUMBER, DOMAIN_NUMBER, OBS_MAX), 1.0, 6.0, ((0, 8), (1, 4)))
    departure = normal_values(seeds[2], (DOMAIN_NUMBER, OBS_MAX), 3.0, 18.0, ((0, 32),), jnp.float32)
    precision_factor = jnp.clip(jnp.exp(math.log(0.5) - 3.218876 * jax.random.uniform(seeds[3], (DOMAIN_NUMBER, OBS_MAX), jnp.float32) ** block_scale(seeds[3], (DOMAIN_NUMBER, OBS_MAX), ((0, 32),), -0.2, 0.2)), 0.02, 0.5)
    measured_lines = draw_measured_lines(jax.random.fold_in(seeds[5], 71), 0)
    return dict(prior_members=prior_members, mapped_prior=mapped_prior, departure=departure, precision_factor=precision_factor, measured_lines=measured_lines)


highest = lax.Precision.HIGHEST

def local_posterior(prior_local_members, measurement_data, departure_line, line_precision_list, lines_in_play):
    grid_quantities = prior_local_members.astype(jnp.float32)
    center = lax.optimization_barrier(jnp.mean(grid_quantities, axis=0))
    spread = grid_quantities - center[None, :]
    values = measurement_data.astype(jnp.float32)
    deviat = values - lax.optimization_barrier(jnp.mean(values, axis=0, keepdims=True))
    row_ids = jnp.arange(OBS_MAX, dtype=jnp.int32)
    weights = jnp.where(row_ids < lines_in_play, line_precision_list, jnp.float32(0.0))
    weighted = deviat * weights[None, :]
    gram_total = jnp.dot(weighted, deviat.T, precision=highest)
    pull_vec = jnp.dot(weighted, departure_line, precision=highest)
    identity = jnp.eye(MEMBER_NUMBER, dtype=jnp.float32)
    system = gram_total + jnp.float32(MEMBER_NUMBER - 1) * identity
    fro_scale = jnp.sqrt(jnp.sum(system * system))
    iterate = system / fro_scale
    inv_root = identity
    for sweep in range(ITERS):
        factor = 0.5 * (3.0 * identity - jnp.dot(inv_root, iterate, precision=highest))
        iterate = jnp.dot(iterate, factor, precision=highest)
        inv_root = jnp.dot(factor, inv_root, precision=highest)
    inner = jnp.dot(inv_root, pull_vec, precision=highest)
    mean_shift = jnp.dot(inv_root, inner, precision=highest) / fro_scale
    transform = math.sqrt(MEMBER_NUMBER - 1) / jnp.sqrt(fro_scale) * inv_root + mean_shift[:, None]
    result = center[None, :] + jnp.dot(transform.T, spread, precision=highest)
    return result.astype(jnp.bfloat16)

def reference(prior_members, mapped_prior, departure, precision_factor, measured_lines):

    def patch_case(domain_number):
        return local_posterior(prior_members[:, domain_number], mapped_prior[:, domain_number], departure[domain_number], precision_factor[domain_number], measured_lines[domain_number])
    result = lax.map(patch_case, jnp.arange(DOMAIN_NUMBER, dtype=jnp.int32))
    return jnp.transpose(result, (1, 0, 2))
```

```python
import functools
import math

import jax
import jax.numpy as jnp
from jax import lax
from jax.experimental import pallas as pl
from jax.experimental.pallas import tpu as pltpu
from jax.sharding import PartitionSpec as P

ITERS = 5
BF16 = jnp.bfloat16
F32 = jnp.float32

VMEM = pl.BlockSpec(memory_space=pltpu.VMEM)
SMEM = pl.BlockSpec(memory_space=pltpu.SMEM)


def mm(a, b, contract=(1, 0)):
    dims = (((contract[0],), (contract[1],)), ((), ()))
    return lax.dot_general(a, b, dims, preferred_element_type=F32)


def split(x):
    high = x.astype(BF16)
    return high, (x - high.astype(F32)).astype(BF16)


def mm3(a, b):
    (ah, al), (bh, bl) = split(a), split(b)
    return mm(ah, bh) + (mm(al, bh) + mm(ah, bl))


def analysis_kernel(unknowns, lines_ref, departure_ref, precision_ref, block_ref, out_ref):
    members = block_ref.shape[0]
    state = block_ref[:, :unknowns].astype(F32)
    values = block_ref[:, unknowns:].astype(F32)
    center = jnp.mean(state, axis=0, keepdims=True)
    spread = state - center
    deviat = values - jnp.mean(values, axis=0, keepdims=True)
    row_ids = lax.broadcasted_iota(jnp.int32, precision_ref.shape, 1)
    weights = jnp.where(row_ids < lines_ref[0], precision_ref[...], 0.0)
    root_weights = jnp.sqrt(weights)
    scaled = deviat * root_weights
    half = scaled.astype(BF16)
    gram = mm(half, half, (1, 1))
    pull = jnp.sum(scaled * (root_weights * departure_ref[...]), axis=1, keepdims=True)

    rows = lax.broadcasted_iota(jnp.int32, (members, members), 0)
    columns = lax.broadcasted_iota(jnp.int32, (members, members), 1)
    system = gram + jnp.where(rows == columns, F32(members - 1), 0.0)
    norm2 = jnp.sum(jnp.sum(system * system, axis=0, keepdims=True), axis=1, keepdims=True)
    inv_scale = lax.rsqrt(norm2)
    iterate = system * inv_scale
    eye15 = jnp.where(rows == columns, F32(1.5), 0.0)
    low = iterate.astype(BF16)
    root = eye15 - 0.5 * iterate
    iterate = 1.5 * iterate - 0.5 * mm(low, low)
    for sweep in range(1, ITERS - 1):
        root_low, iterate_low = root.astype(BF16), iterate.astype(BF16)
        product = mm(root_low, iterate_low).astype(BF16)
        iterate = 1.5 * iterate - 0.5 * mm(iterate_low, product)
        root = 1.5 * root - 0.5 * mm(product, root_low)
    product = mm(root.astype(BF16), iterate.astype(BF16))
    right = jnp.concatenate([spread, jnp.broadcast_to(pull, (members, 128))], axis=1)
    right = mm3(root, right)
    right = 1.5 * right - 0.5 * mm3(product, right)
    moved = right[:, :unknowns]
    shift = jnp.sum(moved * right[:, unknowns : unknowns + 1], axis=0, keepdims=True) * inv_scale
    gain = math.sqrt(members - 1) * jnp.sqrt(inv_scale)
    out_ref[...] = (gain * moved + (center + shift)).astype(BF16)


def local(prior_members, mapped_prior, departure, precision_factor, measured_lines, *, devices):
    own, patches, unknowns = prior_members.shape
    rows = mapped_prior.shape[2]
    members = own * devices
    each = patches // devices
    packed = jnp.concatenate([prior_members, mapped_prior], axis=2)
    packed = jnp.transpose(packed, (1, 0, 2))
    packed = lax.all_to_all(packed, "mem", split_axis=0, concat_axis=0, tiled=True)
    packed = packed.reshape(devices, each, own, unknowns + rows)
    kernel = pl.pallas_call(
        functools.partial(analysis_kernel, unknowns),
        out_shape=jax.ShapeDtypeStruct((members, unknowns), BF16),
        in_specs=[SMEM, VMEM, VMEM, VMEM],
        out_specs=VMEM,
        compiler_params=pltpu.CompilerParams(vmem_limit_bytes=16 << 20),
    )
    results = [
        kernel(
            measured_lines[k : k + 1],
            departure[k : k + 1],
            precision_factor[k : k + 1],
            packed[:, k].reshape(members, unknowns + rows),
        )
        for k in range(each)
    ]
    analysed = jnp.stack([r.reshape(devices, own, unknowns) for r in results], axis=1)
    analysed = analysed.reshape(patches, own, unknowns)
    analysed = lax.all_to_all(analysed, "mem", split_axis=0, concat_axis=0, tiled=True)
    return jnp.transpose(analysed, (1, 0, 2))


def solution(mesh):
    in_specs = (
        P("mem", "grp", None),
        P("mem", "grp", None),
        P(("grp", "mem"), None),
        P(("grp", "mem"), None),
        P(("grp", "mem")),
    )
    body = functools.partial(local, devices=mesh.shape["mem"])
    return jax.shard_map(
        body, mesh=mesh, in_specs=in_specs, out_specs=P("mem", "grp", None), check_vma=False
    )
```

```python
import functools
import math

import jax
import jax.numpy as jnp
from jax import lax
from jax.experimental import pallas as pl
from jax.experimental.pallas import tpu as pltpu
from jax.sharding import PartitionSpec as P


ITERS = 5
PAIRWISE_LIMIT = 16
BF16 = jnp.bfloat16
F32 = jnp.float32

VMEM = pl.BlockSpec(memory_space=pltpu.VMEM)
SMEM = pl.BlockSpec(memory_space=pltpu.SMEM)
HBM = pl.BlockSpec(memory_space=pltpu.HBM)
PARAMS = pltpu.CompilerParams(vmem_limit_bytes=16 << 20)


def mm(a, b, contract=(1, 0)):
    dims = (((contract[0],), (contract[1],)), ((), ()))
    return lax.dot_general(a, b, dims, preferred_element_type=F32)


def split(x):
    high = x.astype(BF16)
    return high, (x - high.astype(F32)).astype(BF16)


def mm3(a, b):
    (ah, al), (bh, bl) = split(a), split(b)
    return mm(ah, bh) + (mm(al, bh) + mm(ah, bl))


def pack_kernel(me_ref, prior_ref, mapped_ref, *refs):
    own, patches, unknowns = prior_ref.shape
    out_refs, (prior_vmem, mapped_vmem, sems) = refs[:-3], refs[-3:]
    mapped_copy = pltpu.make_async_copy(mapped_ref, mapped_vmem, sems.at[0])
    prior_copy = pltpu.make_async_copy(prior_ref, prior_vmem, sems.at[1])
    mapped_copy.start()
    prior_copy.start()
    size = own * patches
    row = lax.broadcasted_iota(jnp.int32, (size, size), 0)
    column = lax.broadcasted_iota(jnp.int32, (size, size), 1)
    target = (row % own) * patches + ((row // own) ^ me_ref[0])
    pick = jnp.where(column == target, F32(1), F32(0)).astype(BF16)
    for source, place, copy in ((mapped_vmem, unknowns, mapped_copy), (prior_vmem, 0, prior_copy)):
        width = source.shape[2]
        copy.wait()
        moved = mm(pick, source[...].reshape(size, width)).astype(BF16)
        for s, out_ref in enumerate(out_refs):
            out_ref[:, place : place + width] = moved[s * own : (s + 1) * own]


def analysis_kernel(unknowns, me_ref, lines_ref, departure_ref, precision_ref, *refs):
    block_refs, out_ref = refs[:-1], refs[-1]
    block = jnp.concatenate([r[...] for r in block_refs], axis=0)
    members = block.shape[0]
    state = block[:, :unknowns].astype(F32)
    values = block[:, unknowns:].astype(F32)
    center = jnp.mean(state, axis=0, keepdims=True)
    spread = state - center
    deviat = values - jnp.mean(values, axis=0, keepdims=True)
    row_ids = lax.broadcasted_iota(jnp.int32, precision_ref.shape, 1)
    weights = jnp.where(row_ids < lines_ref[0], precision_ref[...], 0.0)
    root_weights = jnp.sqrt(weights)
    scaled = deviat * root_weights
    half = scaled.astype(BF16)
    gram = mm(half, half, (1, 1))
    pull = jnp.sum(scaled * (root_weights * departure_ref[...]), axis=1, keepdims=True)

    rows = lax.broadcasted_iota(jnp.int32, (members, members), 0)
    columns = lax.broadcasted_iota(jnp.int32, (members, members), 1)
    system = gram + jnp.where(rows == columns, F32(members - 1), 0.0)
    norm2 = jnp.sum(jnp.sum(system * system, axis=0, keepdims=True), axis=1, keepdims=True)
    inv_scale = lax.rsqrt(norm2)
    iterate = system * inv_scale
    low = iterate.astype(BF16)
    root = jnp.where(rows == columns, F32(1.5), 0.0) - 0.5 * iterate
    iterate = 1.5 * iterate - 0.5 * mm(low, low)
    for _ in range(1, ITERS - 1):
        root_low, iterate_low = root.astype(BF16), iterate.astype(BF16)
        product = mm(root_low, iterate_low).astype(BF16)
        iterate = 1.5 * iterate - 0.5 * mm(iterate_low, product)
        root = 1.5 * root - 0.5 * mm(product, root_low)
    product = mm(root.astype(BF16), iterate.astype(BF16))
    right = jnp.concatenate([spread, jnp.broadcast_to(pull, (members, 128))], axis=1)
    right = mm3(root, right)
    right = 1.5 * right - 0.5 * mm3(product, right)
    moved = right[:, :unknowns]
    shift = jnp.sum(moved * right[:, unknowns : unknowns + 1], axis=0, keepdims=True) * inv_scale
    gain = math.sqrt(members - 1) * jnp.sqrt(inv_scale)
    result = (gain * moved + (center + shift)).astype(BF16)
    if len(block_refs) == 1:
        out_ref[...] = result
    else:
        own = members // len(block_refs)
        for s in range(len(block_refs)):
            out_ref[me_ref[0] ^ s] = result[s * own : (s + 1) * own]


def analyse(me, lines, departure, precision, blocks, unknowns):
    members = sum(b.shape[0] for b in blocks)
    shape = (members, unknowns)
    if len(blocks) > 1:
        shape = (len(blocks), members // len(blocks), unknowns)
    return pl.pallas_call(
        functools.partial(analysis_kernel, unknowns),
        out_shape=jax.ShapeDtypeStruct(shape, BF16),
        in_specs=[SMEM, SMEM, VMEM, VMEM] + [VMEM] * len(blocks),
        out_specs=VMEM,
        compiler_params=PARAMS,
    )(me, lines, departure, precision, *blocks)


def local_pairs(prior_members, mapped_prior, departure, precision_factor, measured_lines, *, devices):
    own, _, unknowns = prior_members.shape
    width = unknowns + mapped_prior.shape[2]
    me = lax.axis_index("mem").astype(jnp.int32).reshape(1)
    blocks = pl.pallas_call(
        pack_kernel,
        out_shape=[jax.ShapeDtypeStruct((own, width), BF16)] * devices,
        in_specs=[SMEM, HBM, HBM],
        out_specs=[VMEM] * devices,
        scratch_shapes=[
            pltpu.VMEM(prior_members.shape, BF16),
            pltpu.VMEM(mapped_prior.shape, BF16),
            pltpu.SemaphoreType.DMA((2,)),
        ],
        compiler_params=PARAMS,
    )(
        me,
        pltpu.with_memory_space_constraint(prior_members, pltpu.HBM),
        pltpu.with_memory_space_constraint(mapped_prior, pltpu.HBM),
    )
    arrived = [blocks[0]]
    for s in range(1, devices):
        pairs = [(a, a ^ s) for a in range(devices)]
        arrived.append(lax.ppermute(blocks[s], "mem", pairs))
    result = analyse(me, measured_lines, departure, precision_factor, arrived, unknowns)
    result = lax.all_to_all(result, "mem", split_axis=0, concat_axis=0, tiled=True)
    return jnp.transpose(result, (1, 0, 2))


def local_any(prior_members, mapped_prior, departure, precision_factor, measured_lines, *, devices):
    own, patches, unknowns = prior_members.shape
    rows = mapped_prior.shape[2]
    each = patches // devices
    packed = jnp.concatenate([prior_members, mapped_prior], axis=2)
    packed = jnp.transpose(packed, (1, 0, 2))
    packed = lax.all_to_all(packed, "mem", split_axis=0, concat_axis=0, tiled=True)
    packed = packed.reshape(devices, each, own, unknowns + rows)
    me = jnp.zeros((1,), jnp.int32)
    results = []
    for k in range(each):
        at = slice(k, k + 1)
        block = packed[:, k].reshape(devices * own, unknowns + rows)
        result = analyse(
            me, measured_lines[at], departure[at], precision_factor[at], [block], unknowns
        )
        results.append(result.reshape(devices, own, unknowns))
    result = jnp.stack(results, axis=1).reshape(patches, own, unknowns)
    result = lax.all_to_all(result, "mem", split_axis=0, concat_axis=0, tiled=True)
    return jnp.transpose(result, (1, 0, 2))


def solution(mesh):
    devices = mesh.shape["mem"]
    in_specs = (
        P("mem", "grp", None),
        P("mem", "grp", None),
        P(("grp", "mem"), None),
        P(("grp", "mem"), None),
        P(("grp", "mem")),
    )

    def step(prior_members, mapped_prior, departure, precision_factor, measured_lines):
        each = departure.shape[0] // mesh.size
        pairwise = each == 1 and devices <= PAIRWISE_LIMIT and devices & (devices - 1) == 0
        body = functools.partial(local_pairs if pairwise else local_any, devices=devices)
        return jax.shard_map(
            body, mesh=mesh, in_specs=in_specs, out_specs=P("mem", "grp", None), check_vma=False
        )(prior_members, mapped_prior, departure, precision_factor, measured_lines)

    return step
```

```python
import functools
import math

import jax
import jax.numpy as jnp
from jax import lax
from jax.experimental import pallas as pl
from jax.experimental.pallas import tpu as pltpu
from jax.sharding import PartitionSpec as P


ITERS = 5
PAIRWISE_LIMIT = 16
ROUNDS = (
    (6, 7, 4, 5, 2, 3, 0, 1),
    (5, 4, 6, 7, 1, 0, 2, 3),
    (3, 6, 7, 0, 5, 4, 1, 2),
    (7, 3, 5, 1, 6, 2, 4, 0),
    (4, 2, 1, 6, 0, 7, 3, 5),
    (1, 0, 3, 2, 7, 6, 5, 4),
    (2, 5, 0, 4, 3, 1, 7, 6),
)
BF16 = jnp.bfloat16
F32 = jnp.float32

VMEM = pl.BlockSpec(memory_space=pltpu.VMEM)
SMEM = pl.BlockSpec(memory_space=pltpu.SMEM)
HBM = pl.BlockSpec(memory_space=pltpu.HBM)
PARAMS = pltpu.CompilerParams(vmem_limit_bytes=16 << 20)


def mm(a, b, contract=(1, 0)):
    dims = (((contract[0],), (contract[1],)), ((), ()))
    return lax.dot_general(a, b, dims, preferred_element_type=F32)


def split(x):
    high = x.astype(BF16)
    return high, (x - high.astype(F32)).astype(BF16)


def mm3(a, b):
    (ah, al), (bh, bl) = split(a), split(b)
    return mm(ah, bh) + (mm(al, bh) + mm(ah, bl))


def partner_of(partners, me):
    found = jnp.int32(partners[0])
    for d in range(1, len(partners)):
        found = jnp.where(me == d, jnp.int32(partners[d]), found)
    return found


def rounds_of(devices):
    if devices == len(ROUNDS) + 1:
        return ROUNDS
    return [[a ^ k for a in range(devices)] for k in range(devices - 1, 0, -1)]


def pack_kernel(me_ref, prior_ref, mapped_ref, *refs):
    own, patches, unknowns = prior_ref.shape
    out_refs, (prior_vmem, mapped_vmem, sems) = refs[:-3], refs[-3:]
    mapped_copy = pltpu.make_async_copy(mapped_ref, mapped_vmem, sems.at[0])
    prior_copy = pltpu.make_async_copy(prior_ref, prior_vmem, sems.at[1])
    mapped_copy.start()
    prior_copy.start()
    size = own * patches
    row = lax.broadcasted_iota(jnp.int32, (size, size), 0)
    column = lax.broadcasted_iota(jnp.int32, (size, size), 1)
    block = row // own
    patch = jnp.full(row.shape, me_ref[0])
    for k, partners in enumerate(rounds_of(patches)):
        patch = jnp.where(block == k + 1, partner_of(partners, me_ref[0]), patch)
    target = (row % own) * patches + patch
    pick = jnp.where(column == target, F32(1), F32(0)).astype(BF16)
    for source, place, copy in ((mapped_vmem, unknowns, mapped_copy), (prior_vmem, 0, prior_copy)):
        width = source.shape[2]
        copy.wait()
        moved = mm(pick, source[...].reshape(size, width)).astype(BF16)
        for s, out_ref in enumerate(out_refs):
            out_ref[:, place : place + width] = moved[s * own : (s + 1) * own]


def analysis_kernel(unknowns, me_ref, lines_ref, departure_ref, precision_ref, *refs):
    block_refs, out_ref = refs[:-1], refs[-1]
    block = jnp.concatenate([r[...] for r in block_refs], axis=0)
    members = block.shape[0]
    state = block[:, :unknowns].astype(F32)
    values = block[:, unknowns:].astype(F32)
    center = jnp.mean(state, axis=0, keepdims=True)
    spread = state - center
    deviat = values - jnp.mean(values, axis=0, keepdims=True)
    row_ids = lax.broadcasted_iota(jnp.int32, precision_ref.shape, 1)
    weights = jnp.where(row_ids < lines_ref[0], precision_ref[...], 0.0)
    root_weights = jnp.sqrt(weights)
    scaled = deviat * root_weights
    half = scaled.astype(BF16)
    gram = mm(half, half, (1, 1))
    pull = jnp.sum(scaled * (root_weights * departure_ref[...]), axis=1, keepdims=True)

    rows = lax.broadcasted_iota(jnp.int32, (members, members), 0)
    columns = lax.broadcasted_iota(jnp.int32, (members, members), 1)

    def to_column(row):
        return jnp.sum(jnp.where(rows == columns, row, 0.0), axis=1, keepdims=True)

    system = gram + jnp.where(rows == columns, F32(members - 1), 0.0)
    norm2 = jnp.sum(jnp.sum(system * system, axis=0, keepdims=True), axis=1, keepdims=True)
    inv_scale = lax.rsqrt(norm2)
    iterate = system * inv_scale
    low = system.astype(BF16)
    square = mm(low, low) * (inv_scale * inv_scale)
    root = jnp.where(rows == columns, F32(1.5), 0.0) - 0.5 * iterate
    iterate = 1.5 * iterate - 0.5 * square
    for _ in range(1, ITERS - 1):
        root_low, iterate_low = root.astype(BF16), iterate.astype(BF16)
        product = mm(root_low, iterate_low).astype(BF16)
        iterate = 1.5 * iterate - 0.5 * mm(iterate_low, product)
        root = 1.5 * root - 0.5 * mm(product, root_low)
    product = mm(root.astype(BF16), iterate.astype(BF16))
    right = mm3(root, spread)
    rest = jnp.where(rows == columns, F32(0.25), 0.0) - 0.5 * product
    moved = 1.25 * right + mm(rest.astype(BF16), right.astype(BF16))
    pull = to_column(jnp.sum(root * pull, axis=0, keepdims=True))
    pull = 1.5 * pull - 0.5 * to_column(jnp.sum(product * pull, axis=0, keepdims=True))
    shift = jnp.sum(moved * pull, axis=0, keepdims=True) * inv_scale
    gain = math.sqrt(members - 1) * jnp.sqrt(inv_scale)
    result = (gain * moved + (center + shift)).astype(BF16)
    if len(block_refs) == 1:
        out_ref[...] = result
    else:
        own = members // len(block_refs)
        out_ref[me_ref[0]] = result[:own]
        for k, partners in enumerate(rounds_of(len(block_refs)), start=1):
            out_ref[partner_of(partners, me_ref[0])] = result[k * own : (k + 1) * own]


def analyse(me, lines, departure, precision, blocks, unknowns):
    members = sum(b.shape[0] for b in blocks)
    shape = (members, unknowns)
    if len(blocks) > 1:
        shape = (len(blocks), members // len(blocks), unknowns)
    return pl.pallas_call(
        functools.partial(analysis_kernel, unknowns),
        out_shape=jax.ShapeDtypeStruct(shape, BF16),
        in_specs=[SMEM, SMEM, VMEM, VMEM] + [VMEM] * len(blocks),
        out_specs=VMEM,
        compiler_params=PARAMS,
    )(me, lines, departure, precision, *blocks)


def local_pairs(prior_members, mapped_prior, departure, precision_factor, measured_lines, *, devices):
    own, _, unknowns = prior_members.shape
    width = unknowns + mapped_prior.shape[2]
    me = lax.axis_index("mem").astype(jnp.int32).reshape(1)
    blocks = pl.pallas_call(
        pack_kernel,
        out_shape=[jax.ShapeDtypeStruct((own, width), BF16)] * devices,
        in_specs=[SMEM, HBM, HBM],
        out_specs=[VMEM] * devices,
        scratch_shapes=[
            pltpu.VMEM(prior_members.shape, BF16),
            pltpu.VMEM(mapped_prior.shape, BF16),
            pltpu.SemaphoreType.DMA((2,)),
        ],
        compiler_params=PARAMS,
    )(
        me,
        pltpu.with_memory_space_constraint(prior_members, pltpu.HBM),
        pltpu.with_memory_space_constraint(mapped_prior, pltpu.HBM),
    )
    arrived = [blocks[0]]
    for k, partners in enumerate(rounds_of(devices), start=1):
        arrived.append(lax.ppermute(blocks[k], "mem", list(enumerate(partners))))
    result = analyse(me, measured_lines, departure, precision_factor, arrived, unknowns)
    result = lax.all_to_all(result, "mem", split_axis=0, concat_axis=0, tiled=True)
    return jnp.transpose(result, (1, 0, 2))


def local_any(prior_members, mapped_prior, departure, precision_factor, measured_lines, *, devices):
    own, patches, unknowns = prior_members.shape
    rows = mapped_prior.shape[2]
    each = patches // devices
    packed = jnp.concatenate([prior_members, mapped_prior], axis=2)
    packed = jnp.transpose(packed, (1, 0, 2))
    packed = lax.all_to_all(packed, "mem", split_axis=0, concat_axis=0, tiled=True)
    packed = packed.reshape(devices, each, own, unknowns + rows)
    me = jnp.zeros((1,), jnp.int32)
    results = []
    for k in range(each):
        at = slice(k, k + 1)
        block = packed[:, k].reshape(devices * own, unknowns + rows)
        result = analyse(
            me, measured_lines[at], departure[at], precision_factor[at], [block], unknowns
        )
        results.append(result.reshape(devices, own, unknowns))
    result = jnp.stack(results, axis=1).reshape(patches, own, unknowns)
    result = lax.all_to_all(result, "mem", split_axis=0, concat_axis=0, tiled=True)
    return jnp.transpose(result, (1, 0, 2))


def solution(mesh):
    devices = mesh.shape["mem"]
    in_specs = (
        P("mem", "grp", None),
        P("mem", "grp", None),
        P(("grp", "mem"), None),
        P(("grp", "mem"), None),
        P(("grp", "mem")),
    )

    def step(prior_members, mapped_prior, departure, precision_factor, measured_lines):
        each = departure.shape[0] // mesh.size
        pairwise = each == 1 and devices <= PAIRWISE_LIMIT and devices & (devices - 1) == 0
        body = functools.partial(local_pairs if pairwise else local_any, devices=devices)
        return jax.shard_map(
            body, mesh=mesh, in_specs=in_specs, out_specs=P("mem", "grp", None), check_vma=False
        )(prior_members, mapped_prior, departure, precision_factor, measured_lines)

    return step
```

```python
import functools
import math

import jax
import jax.numpy as jnp
from jax import lax
from jax.experimental import pallas as pl
from jax.experimental.pallas import tpu as pltpu
from jax.sharding import PartitionSpec as P


ITERS = 5
PAIRWISE_LIMIT = 16
ROUNDS = (
    (6, 7, 4, 5, 2, 3, 0, 1),
    (5, 4, 6, 7, 1, 0, 2, 3),
    (3, 6, 7, 0, 5, 4, 1, 2),
    (7, 3, 5, 1, 6, 2, 4, 0),
    (4, 2, 1, 6, 0, 7, 3, 5),
    (1, 0, 3, 2, 7, 6, 5, 4),
    (2, 5, 0, 4, 3, 1, 7, 6),
)
BF16 = jnp.bfloat16
F32 = jnp.float32

VMEM = pl.BlockSpec(memory_space=pltpu.VMEM)
SMEM = pl.BlockSpec(memory_space=pltpu.SMEM)
HBM = pl.BlockSpec(memory_space=pltpu.HBM)
PARAMS = pltpu.CompilerParams(vmem_limit_bytes=16 << 20)


def mm(a, b, contract=(1, 0)):
    dims = (((contract[0],), (contract[1],)), ((), ()))
    return lax.dot_general(a, b, dims, preferred_element_type=F32)


def split(x):
    high = x.astype(BF16)
    return high, (x - high.astype(F32)).astype(BF16)


def left(a, b):
    high, low = split(b)
    return mm(a, high) + mm(a, low)


def right(a, b):
    high, low = split(a)
    return mm(high, b) + mm(low, b)


def mm3(a, b):
    (ah, al), (bh, bl) = split(a), split(b)
    return mm(ah, bh) + (mm(al, bh) + mm(ah, bl))


def partner_of(partners, me):
    found = jnp.int32(partners[0])
    for d in range(1, len(partners)):
        found = jnp.where(me == d, jnp.int32(partners[d]), found)
    return found


def rounds_of(devices):
    if devices == len(ROUNDS) + 1:
        return ROUNDS
    return [[a ^ k for a in range(devices)] for k in range(devices - 1, 0, -1)]


def pack_kernel(me_ref, prior_ref, mapped_ref, *refs):
    own, patches, unknowns = prior_ref.shape
    out_refs, (prior_vmem, mapped_vmem, sems) = refs[:-3], refs[-3:]
    mapped_copy = pltpu.make_async_copy(mapped_ref, mapped_vmem, sems.at[0])
    prior_copy = pltpu.make_async_copy(prior_ref, prior_vmem, sems.at[1])
    mapped_copy.start()
    prior_copy.start()
    size = own * patches
    row = lax.broadcasted_iota(jnp.int32, (size, size), 0)
    column = lax.broadcasted_iota(jnp.int32, (size, size), 1)
    block = row // own
    patch = jnp.full(row.shape, me_ref[0])
    for k, partners in enumerate(rounds_of(patches)):
        patch = jnp.where(block == k + 1, partner_of(partners, me_ref[0]), patch)
    target = (row % own) * patches + patch
    pick = jnp.where(column == target, F32(1), F32(0)).astype(BF16)
    for source, place, copy in ((mapped_vmem, unknowns, mapped_copy), (prior_vmem, 0, prior_copy)):
        width = source.shape[2]
        copy.wait()
        moved = mm(pick, source[...].reshape(size, width)).astype(BF16)
        for s, out_ref in enumerate(out_refs):
            out_ref[:, place : place + width] = moved[s * own : (s + 1) * own]


def analysis_kernel(unknowns, me_ref, lines_ref, departure_ref, precision_ref, *refs):
    block_refs, out_ref = refs[:-1], refs[-1]
    block = jnp.concatenate([r[...] for r in block_refs], axis=0)
    members = block.shape[0]
    state = block[:, :unknowns].astype(F32)
    values = block[:, unknowns:].astype(F32)
    center = jnp.mean(state, axis=0, keepdims=True)
    spread = state - center
    deviat = values - jnp.mean(values, axis=0, keepdims=True)
    row_ids = lax.broadcasted_iota(jnp.int32, precision_ref.shape, 1)
    weights = jnp.where(row_ids < lines_ref[0], precision_ref[...], 0.0)
    root_weights = jnp.sqrt(weights)
    scaled = deviat * root_weights
    scaled = scaled.astype(BF16)
    gram = mm(scaled, scaled, (1, 1))
    pull = scaled.astype(F32) * (root_weights * departure_ref[...])
    pull = jnp.sum(pull, axis=1, keepdims=True)

    rows = lax.broadcasted_iota(jnp.int32, (members, members), 0)
    columns = lax.broadcasted_iota(jnp.int32, (members, members), 1)

    def times(matrix, column):
        row = jnp.sum(matrix * column, axis=0, keepdims=True)
        return jnp.sum(jnp.where(rows == columns, row, 0.0), axis=1, keepdims=True)

    system = gram + jnp.where(rows == columns, F32(members - 1), 0.0)
    norm2 = jnp.sum(jnp.sum(system * system, axis=0, keepdims=True), axis=1, keepdims=True)
    inv_scale = lax.rsqrt(norm2)
    iterate = system * inv_scale
    product = iterate.astype(BF16)
    root = jnp.where(rows == columns, F32(1.5), 0.0) - 0.5 * product.astype(F32)
    iterate = 1.5 * iterate - 0.5 * right(iterate, product)
    for _ in range(1, ITERS - 1):
        product = mm(root.astype(BF16), iterate.astype(BF16)).astype(BF16)
        iterate = 1.5 * iterate - 0.5 * right(iterate, product)
        root = 1.5 * root - 0.5 * left(product, root)
    product = mm3(root, iterate)
    moved = right(root, spread.astype(BF16))
    moved = 1.5 * moved - 0.5 * mm3(product, moved)
    pull = times(root, pull)
    pull = 1.5 * pull - 0.5 * times(product, pull)
    shift = jnp.sum(moved * (pull * inv_scale), axis=0, keepdims=True)
    gain = math.sqrt(members - 1) * jnp.sqrt(inv_scale)
    result = (gain * moved + (center + shift)).astype(BF16)
    if len(block_refs) == 1:
        out_ref[...] = result
    else:
        own = members // len(block_refs)
        out_ref[me_ref[0]] = result[:own]
        for k, partners in enumerate(rounds_of(len(block_refs)), start=1):
            out_ref[partner_of(partners, me_ref[0])] = result[k * own : (k + 1) * own]


def analyse(me, lines, departure, precision, blocks, unknowns):
    members = sum(b.shape[0] for b in blocks)
    shape = (members, unknowns)
    if len(blocks) > 1:
        shape = (len(blocks), members // len(blocks), unknowns)
    return pl.pallas_call(
        functools.partial(analysis_kernel, unknowns),
        out_shape=jax.ShapeDtypeStruct(shape, BF16),
        in_specs=[SMEM, SMEM, VMEM, VMEM] + [VMEM] * len(blocks),
        out_specs=VMEM,
        compiler_params=PARAMS,
    )(me, lines, departure, precision, *blocks)


def local_pairs(prior_members, mapped_prior, departure, precision_factor, measured_lines, *, devices):
    own, _, unknowns = prior_members.shape
    width = unknowns + mapped_prior.shape[2]
    me = lax.axis_index("mem").astype(jnp.int32).reshape(1)
    blocks = pl.pallas_call(
        pack_kernel,
        out_shape=[jax.ShapeDtypeStruct((own, width), BF16)] * devices,
        in_specs=[SMEM, HBM, HBM],
        out_specs=[VMEM] * devices,
        scratch_shapes=[
            pltpu.VMEM(prior_members.shape, BF16),
            pltpu.VMEM(mapped_prior.shape, BF16),
            pltpu.SemaphoreType.DMA((2,)),
        ],
        compiler_params=PARAMS,
    )(
        me,
        pltpu.with_memory_space_constraint(prior_members, pltpu.HBM),
        pltpu.with_memory_space_constraint(mapped_prior, pltpu.HBM),
    )
    arrived = [blocks[0]]
    for k, partners in enumerate(rounds_of(devices), start=1):
        arrived.append(lax.ppermute(blocks[k], "mem", list(enumerate(partners))))
    result = analyse(me, measured_lines, departure, precision_factor, arrived, unknowns)
    result = lax.all_to_all(result, "mem", split_axis=0, concat_axis=0, tiled=True)
    return jnp.transpose(result, (1, 0, 2))


def local_any(prior_members, mapped_prior, departure, precision_factor, measured_lines, *, devices):
    own, patches, unknowns = prior_members.shape
    rows = mapped_prior.shape[2]
    each = patches // devices
    packed = jnp.concatenate([prior_members, mapped_prior], axis=2)
    packed = jnp.transpose(packed, (1, 0, 2))
    packed = lax.all_to_all(packed, "mem", split_axis=0, concat_axis=0, tiled=True)
    packed = packed.reshape(devices, each, own, unknowns + rows)
    me = jnp.zeros((1,), jnp.int32)
    results = []
    for k in range(each):
        at = slice(k, k + 1)
        block = packed[:, k].reshape(devices * own, unknowns + rows)
        result = analyse(
            me, measured_lines[at], departure[at], precision_factor[at], [block], unknowns
        )
        results.append(result.reshape(devices, own, unknowns))
    result = jnp.stack(results, axis=1).reshape(patches, own, unknowns)
    result = lax.all_to_all(result, "mem", split_axis=0, concat_axis=0, tiled=True)
    return jnp.transpose(result, (1, 0, 2))


def solution(mesh):
    devices = mesh.shape["mem"]
    in_specs = (
        P("mem", "grp", None),
        P("mem", "grp", None),
        P(("grp", "mem"), None),
        P(("grp", "mem"), None),
        P(("grp", "mem")),
    )

    def step(prior_members, mapped_prior, departure, precision_factor, measured_lines):
        each = departure.shape[0] // mesh.size
        pairwise = each == 1 and devices <= PAIRWISE_LIMIT and devices & (devices - 1) == 0
        body = functools.partial(local_pairs if pairwise else local_any, devices=devices)
        return jax.shard_map(
            body, mesh=mesh, in_specs=in_specs, out_specs=P("mem", "grp", None), check_vma=False
        )(prior_members, mapped_prior, departure, precision_factor, measured_lines)

    return step
```

```python
import functools
import math

import jax
import jax.numpy as jnp
from jax import lax
from jax.experimental import pallas as pl
from jax.experimental.pallas import tpu as pltpu
from jax.sharding import PartitionSpec as P


ITERS = 5
PAIRWISE_LIMIT = 16
ROUNDS = (
    (6, 7, 4, 5, 2, 3, 0, 1),
    (5, 4, 6, 7, 1, 0, 2, 3),
    (3, 6, 7, 0, 5, 4, 1, 2),
    (7, 3, 5, 1, 6, 2, 4, 0),
    (4, 2, 1, 6, 0, 7, 3, 5),
    (1, 0, 3, 2, 7, 6, 5, 4),
    (2, 5, 0, 4, 3, 1, 7, 6),
)
BF16 = jnp.bfloat16
F32 = jnp.float32

VMEM = pl.BlockSpec(memory_space=pltpu.VMEM)
SMEM = pl.BlockSpec(memory_space=pltpu.SMEM)
HBM = pl.BlockSpec(memory_space=pltpu.HBM)
PARAMS = pltpu.CompilerParams(vmem_limit_bytes=16 << 20)


def mm(a, b, contract=(1, 0)):
    dims = (((contract[0],), (contract[1],)), ((), ()))
    return lax.dot_general(a, b, dims, preferred_element_type=F32)


def split(x):
    high = x.astype(BF16)
    return high, (x - high.astype(F32)).astype(BF16)


def left(a, b):
    high, low = split(b)
    return mm(a, high) + mm(a, low)


def right(a, b):
    high, low = split(a)
    return mm(high, b) + mm(low, b)


def mm3(a, b):
    (ah, al), (bh, bl) = split(a), split(b)
    return mm(ah, bh) + (mm(al, bh) + mm(ah, bl))


def partner_of(partners, me):
    found = jnp.int32(partners[0])
    for d in range(1, len(partners)):
        found = jnp.where(me == d, jnp.int32(partners[d]), found)
    return found


def rounds_of(devices):
    if devices == len(ROUNDS) + 1:
        return ROUNDS
    return [[a ^ k for a in range(devices)] for k in range(devices - 1, 0, -1)]


def pack_kernel(me_ref, prior_ref, mapped_ref, *refs):
    own, patches, unknowns = prior_ref.shape
    out_refs, (prior_vmem, mapped_vmem, sems) = refs[:-3], refs[-3:]
    mapped_copy = pltpu.make_async_copy(mapped_ref, mapped_vmem, sems.at[0])
    prior_copy = pltpu.make_async_copy(prior_ref, prior_vmem, sems.at[1])
    mapped_copy.start()
    prior_copy.start()
    size = own * patches
    row = lax.broadcasted_iota(jnp.int32, (size, size), 0)
    column = lax.broadcasted_iota(jnp.int32, (size, size), 1)
    block = row // own
    patch = jnp.full(row.shape, me_ref[0])
    for k, partners in enumerate(rounds_of(patches)):
        patch = jnp.where(block == k + 1, partner_of(partners, me_ref[0]), patch)
    target = (row % own) * patches + patch
    pick = jnp.where(column == target, F32(1), F32(0)).astype(BF16)
    for source, place, copy in ((mapped_vmem, unknowns, mapped_copy), (prior_vmem, 0, prior_copy)):
        width = source.shape[2]
        copy.wait()
        moved = mm(pick, source[...].reshape(size, width)).astype(BF16)
        for s, out_ref in enumerate(out_refs):
            out_ref[:, place : place + width] = moved[s * own : (s + 1) * own]


def analysis_kernel(unknowns, me_ref, lines_ref, departure_ref, precision_ref, *refs):
    block_refs, out_ref = refs[:-1], refs[-1]
    block = jnp.concatenate([r[...] for r in block_refs], axis=0)
    members = block.shape[0]
    state = block[:, :unknowns].astype(F32)
    values = block[:, unknowns:].astype(F32)
    center = jnp.mean(state, axis=0, keepdims=True)
    spread = state - center
    deviat = values - jnp.mean(values, axis=0, keepdims=True)
    row_ids = lax.broadcasted_iota(jnp.int32, precision_ref.shape, 1)
    weights = jnp.where(row_ids < lines_ref[0], precision_ref[...], 0.0)
    root_weights = jnp.sqrt(weights)
    scaled = deviat * root_weights
    scaled = scaled.astype(BF16)
    gram = mm(scaled, scaled, (1, 1))
    pull = scaled.astype(F32) * (root_weights * departure_ref[...])
    pull = jnp.sum(pull, axis=1, keepdims=True)

    rows = lax.broadcasted_iota(jnp.int32, (members, members), 0)
    columns = lax.broadcasted_iota(jnp.int32, (members, members), 1)

    def times(matrix, column):
        row = jnp.sum(matrix * column, axis=0, keepdims=True)
        return jnp.sum(jnp.where(rows == columns, row, 0.0), axis=1, keepdims=True)

    system = gram + jnp.where(rows == columns, F32(members - 1), 0.0)
    norm2 = jnp.sum(jnp.sum(system * system, axis=0, keepdims=True), axis=1, keepdims=True)
    inv_scale = lax.rsqrt(norm2)
    product = system.astype(BF16)
    square = right(system, product)
    root = jnp.where(rows == columns, F32(1.5), 0.0) - 0.5 * inv_scale * product.astype(F32)
    iterate = inv_scale * (1.5 * system - 0.5 * inv_scale * square)
    for _ in range(1, ITERS - 1):
        product = mm(root.astype(BF16), iterate.astype(BF16)).astype(BF16)
        iterate = 1.5 * iterate - 0.5 * right(iterate, product)
        root = 1.5 * root - 0.5 * left(product, root)
    product = mm3(root, iterate)
    moved = right(root, spread.astype(BF16))
    moved = 1.5 * moved - 0.5 * mm3(product, moved)
    pull = times(root, pull)
    pull = 1.5 * pull - 0.5 * times(product, pull)
    shift = jnp.sum(moved * (pull * inv_scale), axis=0, keepdims=True)
    gain = math.sqrt(members - 1) * jnp.sqrt(inv_scale)
    result = (gain * moved + (center + shift)).astype(BF16)
    if len(block_refs) == 1:
        out_ref[...] = result
    else:
        own = members // len(block_refs)
        out_ref[me_ref[0]] = result[:own]
        for k, partners in enumerate(rounds_of(len(block_refs)), start=1):
            out_ref[partner_of(partners, me_ref[0])] = result[k * own : (k + 1) * own]


def analyse(me, lines, departure, precision, blocks, unknowns):
    members = sum(b.shape[0] for b in blocks)
    shape = (members, unknowns)
    if len(blocks) > 1:
        shape = (len(blocks), members // len(blocks), unknowns)
    return pl.pallas_call(
        functools.partial(analysis_kernel, unknowns),
        out_shape=jax.ShapeDtypeStruct(shape, BF16),
        in_specs=[SMEM, SMEM, VMEM, VMEM] + [VMEM] * len(blocks),
        out_specs=VMEM,
        compiler_params=PARAMS,
    )(me, lines, departure, precision, *blocks)


def local_pairs(prior_members, mapped_prior, departure, precision_factor, measured_lines, *, devices):
    own, _, unknowns = prior_members.shape
    width = unknowns + mapped_prior.shape[2]
    me = lax.axis_index("mem").astype(jnp.int32).reshape(1)
    blocks = pl.pallas_call(
        pack_kernel,
        out_shape=[jax.ShapeDtypeStruct((own, width), BF16)] * devices,
        in_specs=[SMEM, HBM, HBM],
        out_specs=[VMEM] * devices,
        scratch_shapes=[
            pltpu.VMEM(prior_members.shape, BF16),
            pltpu.VMEM(mapped_prior.shape, BF16),
            pltpu.SemaphoreType.DMA((2,)),
        ],
        compiler_params=PARAMS,
    )(
        me,
        pltpu.with_memory_space_constraint(prior_members, pltpu.HBM),
        pltpu.with_memory_space_constraint(mapped_prior, pltpu.HBM),
    )
    arrived = [blocks[0]]
    for k, partners in enumerate(rounds_of(devices), start=1):
        arrived.append(lax.ppermute(blocks[k], "mem", list(enumerate(partners))))
    result = analyse(me, measured_lines, departure, precision_factor, arrived, unknowns)
    result = lax.all_to_all(result, "mem", split_axis=0, concat_axis=0, tiled=True)
    return jnp.transpose(result, (1, 0, 2))


def local_any(prior_members, mapped_prior, departure, precision_factor, measured_lines, *, devices):
    own, patches, unknowns = prior_members.shape
    rows = mapped_prior.shape[2]
    each = patches // devices
    packed = jnp.concatenate([prior_members, mapped_prior], axis=2)
    packed = jnp.transpose(packed, (1, 0, 2))
    packed = lax.all_to_all(packed, "mem", split_axis=0, concat_axis=0, tiled=True)
    packed = packed.reshape(devices, each, own, unknowns + rows)
    me = jnp.zeros((1,), jnp.int32)
    results = []
    for k in range(each):
        at = slice(k, k + 1)
        block = packed[:, k].reshape(devices * own, unknowns + rows)
        result = analyse(
            me, measured_lines[at], departure[at], precision_factor[at], [block], unknowns
        )
        results.append(result.reshape(devices, own, unknowns))
    result = jnp.stack(results, axis=1).reshape(patches, own, unknowns)
    result = lax.all_to_all(result, "mem", split_axis=0, concat_axis=0, tiled=True)
    return jnp.transpose(result, (1, 0, 2))


def solution(mesh):
    devices = mesh.shape["mem"]
    in_specs = (
        P("mem", "grp", None),
        P("mem", "grp", None),
        P(("grp", "mem"), None),
        P(("grp", "mem"), None),
        P(("grp", "mem")),
    )

    def step(prior_members, mapped_prior, departure, precision_factor, measured_lines):
        each = departure.shape[0] // mesh.size
        pairwise = each == 1 and devices <= PAIRWISE_LIMIT and devices & (devices - 1) == 0
        body = functools.partial(local_pairs if pairwise else local_any, devices=devices)
        return jax.shard_map(
            body, mesh=mesh, in_specs=in_specs, out_specs=P("mem", "grp", None), check_vma=False
        )(prior_members, mapped_prior, departure, precision_factor, measured_lines)

    return step
```

```python
import functools
import math

import jax
import jax.numpy as jnp
from jax import lax
from jax.experimental import pallas as pl
from jax.experimental.pallas import tpu as pltpu
from jax.sharding import PartitionSpec as P


ITERS = 5
PAIRWISE_LIMIT = 16
ROUNDS = (
    (6, 7, 4, 5, 2, 3, 0, 1),
    (5, 4, 6, 7, 1, 0, 2, 3),
    (3, 6, 7, 0, 5, 4, 1, 2),
    (7, 3, 5, 1, 6, 2, 4, 0),
    (4, 2, 1, 6, 0, 7, 3, 5),
    (1, 0, 3, 2, 7, 6, 5, 4),
    (2, 5, 0, 4, 3, 1, 7, 6),
)
BF16 = jnp.bfloat16
F32 = jnp.float32

VMEM = pl.BlockSpec(memory_space=pltpu.VMEM)
SMEM = pl.BlockSpec(memory_space=pltpu.SMEM)
HBM = pl.BlockSpec(memory_space=pltpu.HBM)
PARAMS = pltpu.CompilerParams(vmem_limit_bytes=16 << 20)


def mm(a, b, contract=(1, 0)):
    dims = (((contract[0],), (contract[1],)), ((), ()))
    return lax.dot_general(a, b, dims, preferred_element_type=F32)


def split(x):
    high = x.astype(BF16)
    return high, (x - high.astype(F32)).astype(BF16)


def left(a, b):
    high, low = split(b)
    return mm(a, high) + mm(a, low)


def right(a, b):
    high, low = split(a)
    return mm(high, b) + mm(low, b)


def mm3(a, b):
    (ah, al), (bh, bl) = split(a), split(b)
    return mm(ah, bh) + (mm(al, bh) + mm(ah, bl))


def partner_of(partners, me):
    found = jnp.int32(partners[0])
    for d in range(1, len(partners)):
        found = jnp.where(me == d, jnp.int32(partners[d]), found)
    return found


def rounds_of(devices):
    if devices == len(ROUNDS) + 1:
        return ROUNDS
    return [[a ^ k for a in range(devices)] for k in range(devices - 1, 0, -1)]


def pack_kernel(me_ref, prior_ref, mapped_ref, *refs):
    own, patches, unknowns = prior_ref.shape
    out_refs, (prior_vmem, mapped_vmem, sems) = refs[:-3], refs[-3:]
    mapped_copy = pltpu.make_async_copy(mapped_ref, mapped_vmem, sems.at[0])
    prior_copy = pltpu.make_async_copy(prior_ref, prior_vmem, sems.at[1])
    mapped_copy.start()
    prior_copy.start()
    size = own * patches
    row = lax.broadcasted_iota(jnp.int32, (size, size), 0)
    column = lax.broadcasted_iota(jnp.int32, (size, size), 1)
    block = row // own
    patch = jnp.full(row.shape, me_ref[0])
    for k, partners in enumerate(rounds_of(patches)):
        patch = jnp.where(block == k + 1, partner_of(partners, me_ref[0]), patch)
    target = (row % own) * patches + patch
    pick = jnp.where(column == target, F32(1), F32(0)).astype(BF16)
    mapped_copy.wait()
    prior_copy.wait()
    for source, place in ((mapped_vmem, unknowns), (prior_vmem, 0)):
        width = source.shape[2]
        moved = mm(pick, source[...].reshape(size, width)).astype(BF16)
        for s, out_ref in enumerate(out_refs):
            out_ref[:, place : place + width] = moved[s * own : (s + 1) * own]


def analysis_kernel(unknowns, me_ref, lines_ref, departure_ref, precision_ref, *refs):
    block_refs, out_ref = refs[:-1], refs[-1]
    block = jnp.concatenate([r[...] for r in block_refs], axis=0)
    members = block.shape[0]
    state = block[:, :unknowns].astype(F32)
    values = block[:, unknowns:].astype(F32)
    center = jnp.mean(state, axis=0, keepdims=True)
    spread = state - center
    deviat = values - jnp.mean(values, axis=0, keepdims=True)
    row_ids = lax.broadcasted_iota(jnp.int32, precision_ref.shape, 1)
    weights = jnp.where(row_ids < lines_ref[0], precision_ref[...], 0.0)
    root_weights = jnp.sqrt(weights)
    scaled = deviat * root_weights
    scaled = scaled.astype(BF16)
    gram = mm(scaled, scaled, (1, 1))
    pull = scaled.astype(F32) * (root_weights * departure_ref[...])
    pull = jnp.sum(pull, axis=1, keepdims=True)

    rows = lax.broadcasted_iota(jnp.int32, (members, members), 0)
    columns = lax.broadcasted_iota(jnp.int32, (members, members), 1)

    def times(matrix, column):
        row = jnp.sum(matrix * column, axis=0, keepdims=True)
        return jnp.sum(jnp.where(rows == columns, row, 0.0), axis=1, keepdims=True)

    system = gram + jnp.where(rows == columns, F32(members - 1), 0.0)
    norm2 = jnp.sum(jnp.sum(system * system, axis=0, keepdims=True), axis=1, keepdims=True)
    inv_scale = lax.rsqrt(norm2)
    product = system.astype(BF16)
    square = right(system, product)
    root = jnp.where(rows == columns, F32(1.5), 0.0) - 0.5 * inv_scale * product.astype(F32)
    iterate = inv_scale * (1.5 * system - 0.5 * inv_scale * square)
    for _ in range(1, ITERS - 1):
        product = mm(root.astype(BF16), iterate.astype(BF16)).astype(BF16)
        iterate = 1.5 * iterate - 0.5 * right(iterate, product)
        root = 1.5 * root - 0.5 * left(product, root)
    product = mm3(root, iterate)
    moved = right(root, spread.astype(BF16))
    moved = 1.5 * moved - 0.5 * mm3(product, moved)
    pull = times(root, pull)
    pull = 1.5 * pull - 0.5 * times(product, pull)
    shift = jnp.sum(moved * (pull * inv_scale), axis=0, keepdims=True)
    gain = math.sqrt(members - 1) * jnp.sqrt(inv_scale)
    result = (gain * moved + (center + shift)).astype(BF16)
    if len(block_refs) == 1:
        out_ref[...] = result
    else:
        own = members // len(block_refs)
        out_ref[me_ref[0]] = result[:own]
        for k, partners in enumerate(rounds_of(len(block_refs)), start=1):
            out_ref[partner_of(partners, me_ref[0])] = result[k * own : (k + 1) * own]


def analyse(me, lines, departure, precision, blocks, unknowns):
    members = sum(b.shape[0] for b in blocks)
    shape = (members, unknowns)
    if len(blocks) > 1:
        shape = (len(blocks), members // len(blocks), unknowns)
    return pl.pallas_call(
        functools.partial(analysis_kernel, unknowns),
        out_shape=jax.ShapeDtypeStruct(shape, BF16),
        in_specs=[SMEM, SMEM, VMEM, VMEM] + [VMEM] * len(blocks),
        out_specs=VMEM,
        compiler_params=PARAMS,
    )(me, lines, departure, precision, *blocks)


def local_pairs(prior_members, mapped_prior, departure, precision_factor, measured_lines, *, devices):
    own, _, unknowns = prior_members.shape
    width = unknowns + mapped_prior.shape[2]
    me = lax.axis_index("mem").astype(jnp.int32).reshape(1)
    blocks = pl.pallas_call(
        pack_kernel,
        out_shape=[jax.ShapeDtypeStruct((own, width), BF16)] * devices,
        in_specs=[SMEM, HBM, HBM],
        out_specs=[VMEM] * devices,
        scratch_shapes=[
            pltpu.VMEM(prior_members.shape, BF16),
            pltpu.VMEM(mapped_prior.shape, BF16),
            pltpu.SemaphoreType.DMA((2,)),
        ],
        compiler_params=PARAMS,
    )(
        me,
        pltpu.with_memory_space_constraint(prior_members, pltpu.HBM),
        pltpu.with_memory_space_constraint(mapped_prior, pltpu.HBM),
    )
    arrived = [blocks[0]]
    for k, partners in enumerate(rounds_of(devices), start=1):
        arrived.append(lax.ppermute(blocks[k], "mem", list(enumerate(partners))))
    result = analyse(me, measured_lines, departure, precision_factor, arrived, unknowns)
    result = lax.all_to_all(result, "mem", split_axis=0, concat_axis=0, tiled=True)
    return jnp.transpose(result, (1, 0, 2))


def local_any(prior_members, mapped_prior, departure, precision_factor, measured_lines, *, devices):
    own, patches, unknowns = prior_members.shape
    rows = mapped_prior.shape[2]
    each = patches // devices
    packed = jnp.concatenate([prior_members, mapped_prior], axis=2)
    packed = jnp.transpose(packed, (1, 0, 2))
    packed = lax.all_to_all(packed, "mem", split_axis=0, concat_axis=0, tiled=True)
    packed = packed.reshape(devices, each, own, unknowns + rows)
    me = jnp.zeros((1,), jnp.int32)
    results = []
    for k in range(each):
        at = slice(k, k + 1)
        block = packed[:, k].reshape(devices * own, unknowns + rows)
        result = analyse(
            me, measured_lines[at], departure[at], precision_factor[at], [block], unknowns
        )
        results.append(result.reshape(devices, own, unknowns))
    result = jnp.stack(results, axis=1).reshape(patches, own, unknowns)
    result = lax.all_to_all(result, "mem", split_axis=0, concat_axis=0, tiled=True)
    return jnp.transpose(result, (1, 0, 2))


def solution(mesh):
    devices = mesh.shape["mem"]
    in_specs = (
        P("mem", "grp", None),
        P("mem", "grp", None),
        P(("grp", "mem"), None),
        P(("grp", "mem"), None),
        P(("grp", "mem")),
    )

    def step(prior_members, mapped_prior, departure, precision_factor, measured_lines):
        each = departure.shape[0] // mesh.size
        pairwise = each == 1 and devices <= PAIRWISE_LIMIT and devices & (devices - 1) == 0
        body = functools.partial(local_pairs if pairwise else local_any, devices=devices)
        return jax.shard_map(
            body, mesh=mesh, in_specs=in_specs, out_specs=P("mem", "grp", None), check_vma=False
        )(prior_members, mapped_prior, departure, precision_factor, measured_lines)

    return step
```

```python
import functools
import math

import jax
import jax.numpy as jnp
from jax import lax
from jax.experimental import pallas as pl
from jax.experimental.pallas import tpu as pltpu
from jax.sharding import PartitionSpec as P


ITERS = 5
PAIRWISE_LIMIT = 16
ROUNDS = (
    (6, 7, 4, 5, 2, 3, 0, 1),
    (5, 4, 6, 7, 1, 0, 2, 3),
    (3, 6, 7, 0, 5, 4, 1, 2),
    (7, 3, 5, 1, 6, 2, 4, 0),
    (4, 2, 1, 6, 0, 7, 3, 5),
    (1, 0, 3, 2, 7, 6, 5, 4),
    (2, 5, 0, 4, 3, 1, 7, 6),
)
BF16 = jnp.bfloat16
F32 = jnp.float32

VMEM = pl.BlockSpec(memory_space=pltpu.VMEM)
SMEM = pl.BlockSpec(memory_space=pltpu.SMEM)
HBM = pl.BlockSpec(memory_space=pltpu.HBM)
PARAMS = pltpu.CompilerParams(vmem_limit_bytes=16 << 20)


def mm(a, b, contract=(1, 0)):
    dims = (((contract[0],), (contract[1],)), ((), ()))
    return lax.dot_general(a, b, dims, preferred_element_type=F32)


def split(x):
    high = x.astype(BF16)
    return high, (x - high.astype(F32)).astype(BF16)


def left(a, b):
    high, low = split(b)
    return mm(a, high) + mm(a, low)


def right(a, b):
    high, low = split(a)
    return mm(high, b) + mm(low, b)


def mm3(a, b):
    (ah, al), (bh, bl) = split(a), split(b)
    return mm(ah, bh) + (mm(al, bh) + mm(ah, bl))


def partner_of(partners, me):
    found = jnp.int32(partners[0])
    for d in range(1, len(partners)):
        found = jnp.where(me == d, jnp.int32(partners[d]), found)
    return found


def rounds_of(devices):
    if devices == len(ROUNDS) + 1:
        return ROUNDS
    return [[a ^ k for a in range(devices)] for k in range(devices - 1, 0, -1)]


def pack_kernel(me_ref, prior_ref, mapped_ref, *refs):
    own, patches, unknowns = prior_ref.shape
    out_refs, (prior_vmem, mapped_vmem, sems) = refs[:-3], refs[-3:]
    mapped_copy = pltpu.make_async_copy(mapped_ref, mapped_vmem, sems.at[0])
    prior_copy = pltpu.make_async_copy(prior_ref, prior_vmem, sems.at[1])
    mapped_copy.start()
    prior_copy.start()
    size = own * patches
    row = lax.broadcasted_iota(jnp.int32, (size, size), 0)
    column = lax.broadcasted_iota(jnp.int32, (size, size), 1)
    block = row // own
    patch = jnp.full(row.shape, me_ref[0])
    for k, partners in enumerate(rounds_of(patches)):
        patch = jnp.where(block == k + 1, partner_of(partners, me_ref[0]), patch)
    target = (row % own) * patches + patch
    pick = jnp.where(column == target, F32(1), F32(0)).astype(BF16)
    mapped_copy.wait()
    prior_copy.wait()
    for source, place in ((mapped_vmem, unknowns), (prior_vmem, 0)):
        width = source.shape[2]
        moved = mm(pick, source[...].reshape(size, width)).astype(BF16)
        for s, out_ref in enumerate(out_refs):
            out_ref[:, place : place + width] = moved[s * own : (s + 1) * own]


def analysis_kernel(unknowns, me_ref, lines_ref, departure_ref, precision_ref, *refs):
    block_refs, out_ref = refs[:-1], refs[-1]
    block = jnp.concatenate([r[...] for r in block_refs], axis=0)
    members = block.shape[0]
    state = block[:, :unknowns].astype(F32)
    values = block[:, unknowns:].astype(F32)
    center = jnp.mean(state, axis=0, keepdims=True)
    spread = state - center
    deviat = values - jnp.mean(values, axis=0, keepdims=True)
    row_ids = lax.broadcasted_iota(jnp.int32, precision_ref.shape, 1)
    weights = jnp.where(row_ids < lines_ref[0], precision_ref[...], 0.0)
    root_weights = jnp.sqrt(weights)
    scaled = deviat * root_weights
    scaled = scaled.astype(BF16)
    gram = mm(scaled, scaled.T)
    pull = scaled.astype(F32) * (root_weights * departure_ref[...])
    pull = jnp.sum(pull, axis=1, keepdims=True)

    rows = lax.broadcasted_iota(jnp.int32, (members, members), 0)
    columns = lax.broadcasted_iota(jnp.int32, (members, members), 1)

    def times(matrix, column):
        row = jnp.sum(matrix * column, axis=0, keepdims=True)
        return jnp.sum(jnp.where(rows == columns, row, 0.0), axis=1, keepdims=True)

    system = gram + jnp.where(rows == columns, F32(members - 1), 0.0)
    norm2 = jnp.sum(jnp.sum(system * system, axis=0, keepdims=True), axis=1, keepdims=True)
    inv_scale = lax.rsqrt(norm2)
    product = system.astype(BF16)
    square = mm(product, product)
    root = jnp.where(rows == columns, F32(1.5), 0.0) - 0.5 * inv_scale * product.astype(F32)
    iterate = inv_scale * (1.5 * system - 0.5 * inv_scale * square)
    for _ in range(1, ITERS - 1):
        product = mm(root.astype(BF16), iterate.astype(BF16)).astype(BF16)
        iterate = 1.5 * iterate - 0.5 * right(iterate, product)
        root = 1.5 * root - 0.5 * left(product, root)
    product = mm3(root, iterate)
    moved = mm3(root, spread)
    moved = 1.5 * moved - 0.5 * mm3(product, moved)
    pull = times(root, pull)
    pull = 1.5 * pull - 0.5 * times(product, pull)
    shift = jnp.sum(moved * (pull * inv_scale), axis=0, keepdims=True)
    gain = math.sqrt(members - 1) * jnp.sqrt(inv_scale)
    result = (gain * moved + (center + shift)).astype(BF16)
    if len(block_refs) == 1:
        out_ref[...] = result
    else:
        own = members // len(block_refs)
        out_ref[me_ref[0]] = result[:own]
        for k, partners in enumerate(rounds_of(len(block_refs)), start=1):
            out_ref[partner_of(partners, me_ref[0])] = result[k * own : (k + 1) * own]


def analyse(me, lines, departure, precision, blocks, unknowns):
    members = sum(b.shape[0] for b in blocks)
    shape = (members, unknowns)
    if len(blocks) > 1:
        shape = (len(blocks), members // len(blocks), unknowns)
    return pl.pallas_call(
        functools.partial(analysis_kernel, unknowns),
        out_shape=jax.ShapeDtypeStruct(shape, BF16),
        in_specs=[SMEM, SMEM, VMEM, VMEM] + [VMEM] * len(blocks),
        out_specs=VMEM,
        compiler_params=PARAMS,
    )(me, lines, departure, precision, *blocks)


def local_pairs(prior_members, mapped_prior, departure, precision_factor, measured_lines, *, devices):
    own, _, unknowns = prior_members.shape
    width = unknowns + mapped_prior.shape[2]
    me = lax.axis_index("mem").astype(jnp.int32).reshape(1)
    blocks = pl.pallas_call(
        pack_kernel,
        out_shape=[jax.ShapeDtypeStruct((own, width), BF16)] * devices,
        in_specs=[SMEM, HBM, HBM],
        out_specs=[VMEM] * devices,
        scratch_shapes=[
            pltpu.VMEM(prior_members.shape, BF16),
            pltpu.VMEM(mapped_prior.shape, BF16),
            pltpu.SemaphoreType.DMA((2,)),
        ],
        compiler_params=PARAMS,
    )(
        me,
        pltpu.with_memory_space_constraint(prior_members, pltpu.HBM),
        pltpu.with_memory_space_constraint(mapped_prior, pltpu.HBM),
    )
    arrived = [blocks[0]]
    for k, partners in enumerate(rounds_of(devices), start=1):
        arrived.append(lax.ppermute(blocks[k], "mem", list(enumerate(partners))))
    result = analyse(me, measured_lines, departure, precision_factor, arrived, unknowns)
    result = lax.all_to_all(result, "mem", split_axis=0, concat_axis=0, tiled=True)
    return jnp.transpose(result, (1, 0, 2))


def local_any(prior_members, mapped_prior, departure, precision_factor, measured_lines, *, devices):
    own, patches, unknowns = prior_members.shape
    rows = mapped_prior.shape[2]
    each = patches // devices
    packed = jnp.concatenate([prior_members, mapped_prior], axis=2)
    packed = jnp.transpose(packed, (1, 0, 2))
    packed = lax.all_to_all(packed, "mem", split_axis=0, concat_axis=0, tiled=True)
    packed = packed.reshape(devices, each, own, unknowns + rows)
    me = jnp.zeros((1,), jnp.int32)
    results = []
    for k in range(each):
        at = slice(k, k + 1)
        block = packed[:, k].reshape(devices * own, unknowns + rows)
        result = analyse(
            me, measured_lines[at], departure[at], precision_factor[at], [block], unknowns
        )
        results.append(result.reshape(devices, own, unknowns))
    result = jnp.stack(results, axis=1).reshape(patches, own, unknowns)
    result = lax.all_to_all(result, "mem", split_axis=0, concat_axis=0, tiled=True)
    return jnp.transpose(result, (1, 0, 2))


def solution(mesh):
    devices = mesh.shape["mem"]
    in_specs = (
        P("mem", "grp", None),
        P("mem", "grp", None),
        P(("grp", "mem"), None),
        P(("grp", "mem"), None),
        P(("grp", "mem")),
    )

    def step(prior_members, mapped_prior, departure, precision_factor, measured_lines):
        each = departure.shape[0] // mesh.size
        pairwise = each == 1 and devices <= PAIRWISE_LIMIT and devices & (devices - 1) == 0
        body = functools.partial(local_pairs if pairwise else local_any, devices=devices)
        return jax.shard_map(
            body, mesh=mesh, in_specs=in_specs, out_specs=P("mem", "grp", None), check_vma=False
        )(prior_members, mapped_prior, departure, precision_factor, measured_lines)

    return step
```
